32 devices in a mesh: ctx: 16 (over z, x, core), fsdp: 2 (over y).
Axes of the slice: x: 2, y: 2, z: 4, core: 2. Of those that a mesh axis runs over, the one named last changes fastest.
Arguments:
- inputs: float32 [2, 2048, 640], P('fsdp', 'ctx'), may hold values from -6 to 6
- cotangent: float32 [2, 2048, 640], P('fsdp', 'ctx'), may hold values from -6 to 6
- positions: int32 [2, 2048], P('fsdp', 'ctx'), may hold values from 0 to 4094, as said below
- block_map: int32 [32], replicated, may hold values from 0 to 31, as said below
- matrices: float32 [5570560], P(('ctx', 'fsdp'))
- gain_offsets: float32 [3072], P(('ctx', 'fsdp')), as said below
- first_moment: float32 [5570560], P(('ctx', 'fsdp')), may hold values from -40 to 40
- second_moment: float32 [5570560], P(('ctx', 'fsdp')), may hold values from 102.4 to 1638.4
- gain_first: float32 [3072], P(('ctx', 'fsdp')), may hold values from -40 to 40
- gain_second: float32 [3072], P(('ctx', 'fsdp')), may hold values from 102.4 to 1638.4
Outputs:
- outputs: float32 [2, 2048, 640], P('fsdp', 'ctx')
- input_grad: float32 [2, 2048, 640], P('fsdp', 'ctx')
- matrix_grad: float32 [5570560], P(('ctx', 'fsdp'))
- gain_grad: float32 [3072], P(('ctx', 'fsdp'))
- new_matrices: float32 [5570560], P(('ctx', 'fsdp'))
- new_gains: float32 [3072], P(('ctx', 'fsdp'))
- new_first: float32 [5570560], P(('ctx', 'fsdp'))
- new_second: float32 [5570560], P(('ctx', 'fsdp'))
- new_gain_first: float32 [3072], P(('ctx', 'fsdp'))
- new_gain_second: float32 [3072], P(('ctx', 'fsdp'))
The draws below stay inside these ranges and needn't reach their ends.
Inputs may be any that keep to these rules, and one draw needn't show every extreme that they name: block_map is a permutation; storage slots 2 c and 2 c + 1 hold blocks b and 31 - b for some b. Read in causal order, each sequence's positions start at 0 and rise by 1 to 3 from one token to the next; the rises after tokens 2 i and 2 i + 1 sum to 4, so the last token's position is 4094. `gain_offsets`: every entry lies between -0.1 and 0.3.
All inputs are finite; a program needn't handle non-finite values.
Results may differ from the reference program's by a relative error of at most 0.024.
Values may be sent and summed in bfloat16 or wider, within the bound.
A program may use at most 192 MiB of HBM per device.

```python
import math
import jax
import jax.numpy as jnp
from jax import lax

D = 640
HEADS = 4
HD = 256
FF = 2048
BLK = 64
STEP = 3
NBLK = 32
L = 2048
SEQS = 2
NMAT = 5570560
NGAIN = 3072


def pair_map(key):
    half_count = NBLK // 2
    order_draw = jax.random.permutation(jax.random.fold_in(key, 11), half_count).astype(jnp.int32)
    flip_bits = jax.random.randint(jax.random.fold_in(key, 12), (half_count,), 0, 2)
    early_blocks = jnp.where(flip_bits == 1, NBLK - 1 - order_draw, order_draw)
    late_blocks = NBLK - 1 - early_blocks
    return jnp.stack([early_blocks, late_blocks], axis=1).reshape(NBLK).astype(jnp.int32)


def draw_block_map(key, part):
    return pair_map(key)


def draw_positions(key, part):
    mapping = pair_map(key)
    first_rise = jax.random.randint(jax.random.fold_in(key, 13), (SEQS, (L - 2) // 2), 1, 4).astype(jnp.int32)
    paired = jnp.stack([first_rise, 4 - first_rise], axis=2).reshape(SEQS, L - 2)
    steps_up = jnp.concatenate([jnp.zeros((SEQS, 1), jnp.int32), paired, jnp.full((SEQS, 1), 2, jnp.int32)], axis=1)
    seq_positions = jnp.cumsum(steps_up, axis=1).astype(jnp.int32)
    blocks = seq_positions.reshape(SEQS, NBLK, BLK)
    return blocks[:, mapping].reshape(SEQS, L).astype(jnp.int32)


def draw_matrices(key, part):
    index_all = jnp.arange(NMAT)
    first_end = D * (HEADS * HD + 2 * HD)
    second_end = first_end + HEADS * HD * D
    third_end = second_end + 2 * D * FF
    scale_all = jnp.where(index_all < first_end, D ** (-0.5), jnp.where(index_all < second_end, (HEADS * HD) ** (-0.5), jnp.where(index_all < third_end, D ** (-0.5), FF ** (-0.5))))
    raw_draw = jax.random.truncated_normal(key, -3.0, 3.0, (NMAT,), jnp.float32)
    return (raw_draw * scale_all).astype(jnp.float32)


def draw_gain_offsets(key, part):
    index_all = jnp.arange(NGAIN)
    query_key = (index_all >= D) & (index_all < D + 2 * HD)
    base_draw = jax.random.uniform(jax.random.fold_in(key, 21), (NGAIN,), jnp.float32, -0.08, 0.08)
    special = jax.random.uniform(jax.random.fold_in(key, 22), (NGAIN,), jnp.float32, -0.1, 0.3)
    return jnp.where(query_key, special, base_draw).astype(jnp.float32)


def shard_levels(own_key, extent, cuts, least, high):
    loudness, own = 1.0, jax.random.fold_in(own_key, 6)
    for position, parts in cuts:
        steps = jnp.exp(jax.random.uniform(jax.random.fold_in(own, position), (parts,), jnp.float32, least / len(cuts), high / len(cuts)))
        loudness = loudness * jnp.repeat(steps, extent[position] // parts).reshape([-1 if axis == position else 1 for axis in range(len(extent))])
    return loudness


def scatter_about(stream_key, shape, scale, most, shards=(), held_as=jnp.bfloat16):
    values = scale * jax.random.normal(stream_key, shape, jnp.float32)
    if shards:
        values = values * shard_levels(stream_key, shape, shards, -0.22, 0.18)
    return jnp.clip(values, -most, most).astype(held_as)


def setup_inputs(seed: int = 0) -> dict:
    splits = jax.random.split(jax.random.key(seed), 11)
    inputs = scatter_about(splits[0], (SEQS, L, D), 1.0, 6.0, ((0, 2), (1, 16)), jnp.float32)
    cotangent = scatter_about(splits[1], (SEQS, L, D), 1.0, 6.0, ((0, 2), (1, 16)), jnp.float32)
    positions = draw_positions(jax.random.fold_in(splits[10], 71), 0)
    block_map = draw_block_map(jax.random.fold_in(splits[10], 71), 0)
    matrices = draw_matrices(jax.random.fold_in(splits[10], 71), 0)
    gain_offsets = draw_gain_offsets(jax.random.fold_in(splits[10], 71), 0)
    first_moment = scatter_about(splits[6], (NMAT,), (0.1 * (SEQS * L) ** 0.5), 40.0, ((0, 32),), jnp.float32)
    second_moment = jnp.clip(jnp.exp(math.log(1638.4) - 2.7725887 * jax.random.uniform(splits[7], (NMAT,), jnp.float32) ** shard_levels(splits[7], (NMAT,), ((0, 32),), -0.2, 0.2)), 102.4, 1638.4)
    gain_first = scatter_about(splits[8], (NGAIN,), (0.1 * (SEQS * L) ** 0.5), 40.0, ((0, 32),), jnp.float32)
    gain_second = jnp.clip(jnp.exp(math.log(1638.4) - 2.7725887 * jax.random.uniform(splits[9], (NGAIN,), jnp.float32) ** shard_levels(splits[9], (NGAIN,), ((0, 32),), -0.2, 0.2)), 102.4, 1638.4)
    return dict(inputs=inputs, cotangent=cotangent, positions=positions, block_map=block_map, matrices=matrices, gain_offsets=gain_offsets, first_moment=first_moment, second_moment=second_moment, gain_first=gain_first, gain_second=gain_second)


NORM_EPS = 1e-06
ROPE_BASE = 1000000.0
LEARN_RATE = 0.03
BETA_ONE = 0.9
BETA_TWO = 0.95
ADAM_EPS = 1e-08
DECAY_RATE = 0.1

def rms_apply(values, offset):
    scale_rows = lax.rsqrt(lax.optimization_barrier(jnp.mean(values * values, axis=-1, keepdims=True)) + NORM_EPS)
    return values * scale_rows * (1.0 + offset)

def norm_back(values, offset, upstream):
    _, pullback = jax.vjp(rms_apply, values, offset)
    return pullback(upstream)

def gated_unit(gate_values, up_values):
    return jax.nn.gelu(gate_values, approximate=True) * up_values

def rope_tables(token_pos):
    half_width = HD // 2
    exponents = jnp.arange(half_width, dtype=jnp.float32) * (2.0 / HD)
    frequency = jnp.power(jnp.float32(ROPE_BASE), -exponents)
    angles = token_pos.astype(jnp.float32)[:, None] * frequency[None, :]
    cosine_table = jnp.cos(angles)
    sine_table = jnp.sin(angles)
    return (jnp.concatenate([cosine_table, cosine_table], axis=-1), jnp.concatenate([sine_table, sine_table], axis=-1))

def rotate(values, cosine_table, sine_table):
    half_width = values.shape[-1] // 2
    first_half = values[..., :half_width]
    second_half = values[..., half_width:]
    turned = jnp.concatenate([-second_half, first_half], axis=-1)
    return values * cosine_table + turned * sine_table

def rotate_back(upstream, cosine_table, sine_table):
    half_width = upstream.shape[-1] // 2
    weighted = upstream * sine_table
    turned = jnp.concatenate([weighted[..., half_width:], -weighted[..., :half_width]], axis=-1)
    return upstream * cosine_table + turned

def split_weights(flat_values):
    width_qkv = HEADS * HD + 2 * HD
    first_end = D * width_qkv
    second_end = first_end + HEADS * HD * D
    third_end = second_end + 2 * D * FF
    return (flat_values[:first_end].reshape(D, width_qkv), flat_values[first_end:second_end].reshape(HEADS * HD, D), flat_values[second_end:third_end].reshape(D, 2 * FF), flat_values[third_end:].reshape(FF, D))

def split_gains(flat_values):
    return (flat_values[:D], flat_values[D:D + HD], flat_values[D + HD:D + 2 * HD], flat_values[D + 2 * HD:2 * D + 2 * HD], flat_values[2 * D + 2 * HD:3 * D + 2 * HD], flat_values[3 * D + 2 * HD:])

def adamw_update(weights, first_state, second_state, gradient):
    new_first = BETA_ONE * first_state + (1.0 - BETA_ONE) * gradient
    new_second = BETA_TWO * second_state + (1.0 - BETA_TWO) * gradient * gradient
    first_hat = new_first / (1.0 - BETA_ONE ** STEP)
    second_hat = new_second / (1.0 - BETA_TWO ** STEP)
    update = first_hat / (jnp.sqrt(second_hat) + ADAM_EPS) + DECAY_RATE * weights
    return (weights - LEARN_RATE * update, new_first, new_second)

def attend_forward(queries, key_rows, value_rows):
    length = key_rows.shape[0]
    block_rows = length // 16
    key_index = jnp.arange(length, dtype=jnp.int32)
    keys_wide = key_rows.astype(jnp.float32)
    values_wide = value_rows.astype(jnp.float32)

    def one_block(counter):
        first_row = (counter * block_rows).astype(jnp.int32)
        query_block = lax.dynamic_slice_in_dim(queries, first_row, block_rows, 0).astype(jnp.float32)
        query_index = first_row + jnp.arange(block_rows, dtype=jnp.int32)
        scores = jnp.einsum('qhd,kd->qhk', query_block, keys_wide)
        allowed = (key_index[None, :] <= query_index[:, None])[:, None, :]
        masked = jnp.where(allowed, scores, -jnp.inf)
        row_peak = lax.optimization_barrier(jnp.max(masked, axis=-1))
        weights = jnp.exp(masked - row_peak[..., None])
        row_total = lax.optimization_barrier(jnp.sum(weights, axis=-1))
        weights_low = lax.optimization_barrier(weights.astype(jnp.bfloat16)).astype(jnp.float32)
        output = (jnp.einsum('qhk,kd->qhd', weights_low, values_wide) / row_total[..., None]).astype(jnp.bfloat16)
        return (output, row_peak + jnp.log(row_total))
    outputs, log_totals = lax.map(one_block, jnp.arange(16, dtype=jnp.int32))
    return (outputs.reshape(length, HEADS, HD), log_totals.reshape(length, HEADS))

def attend_backward(queries, key_rows, value_rows, outputs, log_totals, grad_out):
    length = key_rows.shape[0]
    block_rows = length // 16
    key_index = jnp.arange(length, dtype=jnp.int32)
    keys_wide = key_rows.astype(jnp.float32)
    values_wide = value_rows.astype(jnp.float32)
    delta_all = lax.optimization_barrier(jnp.sum(grad_out.astype(jnp.float32) * outputs.astype(jnp.float32), axis=-1))

    def one_block(carried, counter):
        key_acc, value_acc = carried
        first_row = (counter * block_rows).astype(jnp.int32)
        query_block = lax.dynamic_slice_in_dim(queries, first_row, block_rows, 0).astype(jnp.float32)
        grad_block = lax.dynamic_slice_in_dim(grad_out, first_row, block_rows, 0).astype(jnp.float32)
        lse_block = lax.dynamic_slice_in_dim(log_totals, first_row, block_rows, 0)
        delta_block = lax.dynamic_slice_in_dim(delta_all, first_row, block_rows, 0)
        query_index = first_row + jnp.arange(block_rows, dtype=jnp.int32)
        scores = jnp.einsum('qhd,kd->qhk', query_block, keys_wide)
        allowed = (key_index[None, :] <= query_index[:, None])[:, None, :]
        probability = jnp.where(allowed, jnp.exp(scores - lse_block[..., None]), 0.0)
        probability_low = lax.optimization_barrier(probability.astype(jnp.bfloat16)).astype(jnp.float32)
        value_acc = value_acc + jnp.einsum('qhk,qhd->kd', probability_low, grad_block)
        grad_prob = jnp.einsum('qhd,kd->qhk', grad_block, values_wide)
        grad_scores = lax.optimization_barrier((probability * (grad_prob - delta_block[..., None])).astype(jnp.bfloat16)).astype(jnp.float32)
        grad_query = jnp.einsum('qhk,kd->qhd', grad_scores, keys_wide)
        key_acc = key_acc + jnp.einsum('qhk,qhd->kd', grad_scores, query_block)
        return ((key_acc, value_acc), grad_query)
    zero_rows = jnp.zeros((length, HD), jnp.float32)
    (key_acc, value_acc), grad_queries = lax.scan(one_block, (zero_rows, zero_rows), jnp.arange(16, dtype=jnp.int32))
    return (grad_queries.reshape(length, HEADS, HD), key_acc, value_acc)

def reference(inputs, cotangent, positions, block_map, matrices, gain_offsets, first_moment, second_moment, gain_first, gain_second):
    gains_low = lax.optimization_barrier(gain_offsets.astype(jnp.bfloat16))
    w_qkv, w_out, w_gateup, w_down = split_weights(matrices.astype(jnp.bfloat16))
    gain_in, gain_query, gain_key, gain_attn, gain_ffn, gain_post = split_gains(gains_low.astype(jnp.float32))
    token_count = SEQS * L
    query_scale = HD ** (-0.5)

    def to_order(values):
        blocks = values.reshape((SEQS, NBLK, BLK) + values.shape[2:])
        placed = jnp.zeros_like(blocks).at[:, block_map].set(blocks)
        return placed.reshape((token_count,) + values.shape[2:])

    def from_order(values):
        blocks = values.reshape((SEQS, NBLK, BLK) + values.shape[1:])
        return blocks[:, block_map].reshape((SEQS, L) + values.shape[1:])
    residual_in = to_order(inputs)
    grad_output = to_order(cotangent)
    token_pos = to_order(positions)
    cosine_table, sine_table = rope_tables(token_pos)
    normed_in = rms_apply(residual_in, gain_in).astype(jnp.bfloat16)
    projected = jnp.dot(normed_in, w_qkv, preferred_element_type=jnp.float32)
    query_raw = projected[:, :HEADS * HD].reshape(token_count, HEADS, HD)
    key_raw = projected[:, HEADS * HD:HEADS * HD + HD]
    value_raw = projected[:, HEADS * HD + HD:]
    query_normed = rms_apply(query_raw, gain_query)
    key_normed = rms_apply(key_raw, gain_key)
    query_all = lax.optimization_barrier((rotate(query_normed, cosine_table[:, None], sine_table[:, None]) * query_scale).astype(jnp.bfloat16))
    key_all = lax.optimization_barrier(rotate(key_normed, cosine_table, sine_table).astype(jnp.bfloat16))
    value_all = lax.optimization_barrier(value_raw.astype(jnp.bfloat16))
    attn_parts = []
    lse_parts = []
    for seq_index in range(SEQS):
        first_row = seq_index * L
        out_part, lse_part = attend_forward(query_all[first_row:first_row + L], key_all[first_row:first_row + L], value_all[first_row:first_row + L])
        attn_parts.append(out_part)
        lse_parts.append(lse_part)
    attn_rows = lax.optimization_barrier(jnp.concatenate(attn_parts, axis=0))
    log_totals = jnp.concatenate(lse_parts, axis=0)
    attn_flat = attn_rows.reshape(token_count, HEADS * HD)
    branch_attn = jnp.dot(attn_flat, w_out, preferred_element_type=jnp.float32)
    after_attn = residual_in + rms_apply(branch_attn, gain_attn)
    normed_mid = rms_apply(after_attn, gain_ffn).astype(jnp.bfloat16)
    gate_up = jnp.dot(normed_mid, w_gateup, preferred_element_type=jnp.float32)
    gate_values = gate_up[:, :FF]
    up_values = gate_up[:, FF:]
    hidden = gated_unit(gate_values, up_values).astype(jnp.bfloat16)
    branch_ffn = jnp.dot(hidden, w_down, preferred_element_type=jnp.float32)
    result = after_attn + rms_apply(branch_ffn, gain_post)
    grad_branch, grad_gain_post = norm_back(branch_ffn, gain_post, grad_output)
    grad_branch_low = grad_branch.astype(jnp.bfloat16)
    grad_down = jnp.dot(hidden.T, grad_branch_low, preferred_element_type=jnp.float32)
    grad_hidden = jnp.dot(grad_branch_low, w_down.T, preferred_element_type=jnp.float32)
    _, unit_pull = jax.vjp(gated_unit, gate_values, up_values)
    grad_gate, grad_up = unit_pull(grad_hidden)
    grad_gateup_low = jnp.concatenate([grad_gate, grad_up], axis=1).astype(jnp.bfloat16)
    grad_gateup = jnp.dot(normed_mid.T, grad_gateup_low, preferred_element_type=jnp.float32)
    grad_normed_mid = jnp.dot(grad_gateup_low, w_gateup.T, preferred_element_type=jnp.float32)
    grad_mid_part, grad_gain_ffn = norm_back(after_attn, gain_ffn, grad_normed_mid)
    grad_after = grad_output + grad_mid_part
    grad_attn_branch, grad_gain_attn = norm_back(branch_attn, gain_attn, grad_after)
    grad_attn_low = grad_attn_branch.astype(jnp.bfloat16)
    grad_wout = jnp.dot(attn_flat.T, grad_attn_low, preferred_element_type=jnp.float32)
    grad_rows = lax.optimization_barrier(jnp.dot(grad_attn_low, w_out.T, preferred_element_type=jnp.float32).astype(jnp.bfloat16)).reshape(token_count, HEADS, HD)
    query_grads = []
    key_grads = []
    value_grads = []
    for seq_index in range(SEQS):
        first_row = seq_index * L
        rows_here = slice(first_row, first_row + L)
        grad_query_part, grad_key_part, grad_value_part = attend_backward(query_all[rows_here], key_all[rows_here], value_all[rows_here], attn_rows[rows_here], log_totals[rows_here], grad_rows[rows_here])
        query_grads.append(grad_query_part)
        key_grads.append(grad_key_part)
        value_grads.append(grad_value_part)
    grad_query_rot = jnp.concatenate(query_grads, axis=0)
    grad_key_rot = jnp.concatenate(key_grads, axis=0)
    grad_value = jnp.concatenate(value_grads, axis=0)
    grad_query_normed = rotate_back(grad_query_rot * query_scale, cosine_table[:, None], sine_table[:, None])
    grad_query_raw, grad_gain_query = norm_back(query_raw, gain_query, grad_query_normed)
    grad_key_normed = rotate_back(grad_key_rot, cosine_table, sine_table)
    grad_key_raw, grad_gain_key = norm_back(key_raw, gain_key, grad_key_normed)
    grad_projected = jnp.concatenate([grad_query_raw.reshape(token_count, HEADS * HD), grad_key_raw, grad_value], axis=1).astype(jnp.bfloat16)
    grad_wqkv = jnp.dot(normed_in.T, grad_projected, preferred_element_type=jnp.float32)
    grad_normed_in = jnp.dot(grad_projected, w_qkv.T, preferred_element_type=jnp.float32)
    grad_in_part, grad_gain_in = norm_back(residual_in, gain_in, grad_normed_in)
    grad_input = grad_after + grad_in_part
    matrix_grad = jnp.concatenate([grad_wqkv.reshape(-1), grad_wout.reshape(-1), grad_gateup.reshape(-1), grad_down.reshape(-1)])
    gain_grad = jnp.concatenate([grad_gain_in, grad_gain_query, grad_gain_key, grad_gain_attn, grad_gain_ffn, grad_gain_post])
    new_matrices, new_first, new_second = adamw_update(matrices, first_moment, second_moment, matrix_grad)
    new_gains, new_gain_first, new_gain_second = adamw_update(gain_offsets, gain_first, gain_second, gain_grad)
    return (from_order(result), from_order(grad_input), matrix_grad, gain_grad, new_matrices, new_gains, new_first, new_second, new_gain_first, new_gain_second)
```

```python
import jax
import jax.numpy as jnp
from jax import lax
from jax.sharding import PartitionSpec as P

D = 640
HEADS = 4
HD = 256
FF = 2048
BLK = 64
STEP = 3
LANES = 128


NORM_EPS = 1e-06
ROPE_BASE = 1000000.0
LEARN_RATE = 0.03
BETA_ONE = 0.9
BETA_TWO = 0.95
ADAM_EPS = 1e-08
DECAY_RATE = 0.1


def rms_apply(values, offset):
    scale_rows = lax.rsqrt(jnp.mean(values * values, axis=-1, keepdims=True) + NORM_EPS)
    return values * scale_rows * (1.0 + offset)


def norm_back(values, offset, upstream):
    _, pullback = jax.vjp(rms_apply, values, offset)
    return pullback(upstream)


def gated_unit(gate_values, up_values):
    return jax.nn.gelu(gate_values, approximate=True) * up_values


def rope_tables(token_pos):
    half_width = HD // 2
    exponents = jnp.arange(half_width, dtype=jnp.float32) * (2.0 / HD)
    frequency = jnp.power(jnp.float32(ROPE_BASE), -exponents)
    angles = token_pos.astype(jnp.float32)[:, None] * frequency[None, :]
    cosine_table = jnp.cos(angles)
    sine_table = jnp.sin(angles)
    return (
        jnp.concatenate([cosine_table, cosine_table], axis=-1),
        jnp.concatenate([sine_table, sine_table], axis=-1),
    )


def rotate(values, cosine_table, sine_table):
    half_width = values.shape[-1] // 2
    first_half = values[..., :half_width]
    second_half = values[..., half_width:]
    turned = jnp.concatenate([-second_half, first_half], axis=-1)
    return values * cosine_table + turned * sine_table


def rotate_back(upstream, cosine_table, sine_table):
    half_width = upstream.shape[-1] // 2
    weighted = upstream * sine_table
    turned = jnp.concatenate([weighted[..., half_width:], -weighted[..., :half_width]], axis=-1)
    return upstream * cosine_table + turned


def split_weights(flat_values):
    width_qkv = HEADS * HD + 2 * HD
    first_end = D * width_qkv
    second_end = first_end + HEADS * HD * D
    third_end = second_end + 2 * D * FF
    return (
        flat_values[:first_end].reshape(D, width_qkv),
        flat_values[first_end:second_end].reshape(HEADS * HD, D),
        flat_values[second_end:third_end].reshape(D, 2 * FF),
        flat_values[third_end:].reshape(FF, D),
    )


def split_gains(flat_values):
    return (
        flat_values[:D],
        flat_values[D : D + HD],
        flat_values[D + HD : D + 2 * HD],
        flat_values[D + 2 * HD : 2 * D + 2 * HD],
        flat_values[2 * D + 2 * HD : 3 * D + 2 * HD],
        flat_values[3 * D + 2 * HD :],
    )


def adamw_update(weights, first_state, second_state, gradient):
    new_first = BETA_ONE * first_state + (1.0 - BETA_ONE) * gradient
    new_second = BETA_TWO * second_state + (1.0 - BETA_TWO) * gradient * gradient
    first_hat = new_first / (1.0 - BETA_ONE**STEP)
    second_hat = new_second / (1.0 - BETA_TWO**STEP)
    update = first_hat / (jnp.sqrt(second_hat) + ADAM_EPS) + DECAY_RATE * weights
    return (weights - LEARN_RATE * update, new_first, new_second)


def tile_forward(carried, query_rows, query_order, key_rows, value_rows, key_order):
    row_peak, row_total, row_accum = carried
    scores = lax.dot_general(
        key_rows, query_rows, (((1,), (1,)), ((), ())), preferred_element_type=jnp.float32
    )
    allowed = key_order[:, None] <= query_order[None, :]
    masked = jnp.where(allowed, scores, -jnp.inf)
    new_peak = jnp.maximum(row_peak, jnp.max(masked, axis=0))
    weights = jnp.exp(masked - new_peak[None, :])
    rescale = jnp.exp(row_peak - new_peak)
    new_total = row_total * rescale + jnp.sum(weights, axis=0)
    weights_low = weights.astype(jnp.bfloat16)
    update = lax.dot_general(
        weights_low, value_rows, (((0,), (0,)), ((), ())), preferred_element_type=jnp.float32
    )
    return (new_peak, new_total, row_accum * rescale[:, None] + update)


def tile_backward(
    query_rows, query_order, grad_rows, log_total, delta_rows, key_rows, value_rows, key_order
):
    scores = lax.dot_general(
        key_rows, query_rows, (((1,), (1,)), ((), ())), preferred_element_type=jnp.float32
    )
    allowed = key_order[:, None] <= query_order[None, :]
    probability = jnp.where(allowed, jnp.exp(scores - log_total[None, :]), 0.0)
    probability_low = probability.astype(jnp.bfloat16)
    value_part = jnp.dot(probability_low, grad_rows, preferred_element_type=jnp.float32)
    grad_prob = lax.dot_general(
        value_rows, grad_rows, (((1,), (1,)), ((), ())), preferred_element_type=jnp.float32
    )
    grad_scores = (probability * (grad_prob - delta_rows[None, :])).astype(jnp.bfloat16)
    query_part = lax.dot_general(
        grad_scores, key_rows, (((0,), (0,)), ((), ())), preferred_element_type=jnp.float32
    )
    key_part = jnp.dot(grad_scores, query_rows, preferred_element_type=jnp.float32)
    return (query_part, jnp.concatenate([key_part, value_part], axis=1))


def add_rows(term_rows, tile_rows, first_row):
    current = lax.dynamic_slice_in_dim(term_rows, first_row, tile_rows.shape[0], 0)
    return lax.dynamic_update_slice_in_dim(term_rows, current + tile_rows, first_row, 0)


def shards(
    inputs,
    cotangent,
    positions,
    block_map,
    matrices,
    gain_offsets,
    first_moment,
    second_moment,
    gain_first,
    gain_second,
):
    gathered = lax.all_gather(
        matrices.astype(jnp.bfloat16).reshape(-1, LANES), ("ctx", "fsdp"), axis=0, tiled=True
    ).reshape(-1)
    gains_low = lax.all_gather(
        gain_offsets.astype(jnp.bfloat16), ("ctx", "fsdp"), axis=0, tiled=True
    )
    w_qkv, w_out, w_gateup, w_down = split_weights(gathered)
    gain_in, gain_query, gain_key, gain_attn, gain_ffn, gain_post = split_gains(
        gains_low.astype(jnp.float32)
    )
    token_rows = inputs.shape[1]
    query_count = token_rows * HEADS
    upper_span = BLK * HEADS
    query_scale = HD ** (-0.5)
    residual_in = inputs[0]
    grad_output = cotangent[0]
    num_blocks = block_map.shape[0]
    block_ids = jnp.arange(num_blocks, dtype=jnp.int32)
    block_offsets = jnp.arange(BLK, dtype=jnp.int32)
    ctx_index = lax.axis_index("ctx")
    own_blocks = jnp.sum(
        jnp.where(
            (2 * ctx_index + jnp.arange(2, dtype=jnp.int32))[:, None] == block_ids[None, :],
            block_map[None, :],
            0,
        ),
        axis=1,
    )
    lower_block = jnp.min(own_blocks)
    upper_block = jnp.max(own_blocks)
    upper_start = jnp.where(own_blocks[1] > own_blocks[0], 1, 0) * upper_span
    token_order = (own_blocks[:, None] * BLK + block_offsets[None, :]).reshape(token_rows)
    query_order = jnp.repeat(token_order, HEADS)
    cosine_table, sine_table = rope_tables(positions[0])
    normed_in = rms_apply(residual_in, gain_in).astype(jnp.bfloat16)
    projected = jnp.dot(normed_in, w_qkv, preferred_element_type=jnp.float32)
    query_raw = projected[:, : HEADS * HD].reshape(token_rows, HEADS, HD)
    key_raw = projected[:, HEADS * HD : HEADS * HD + HD]
    value_raw = projected[:, HEADS * HD + HD :]
    query_normed = rms_apply(query_raw, gain_query)
    key_normed = rms_apply(key_raw, gain_key)
    query_rows = (
        (rotate(query_normed, cosine_table[:, None], sine_table[:, None]) * query_scale)
        .astype(jnp.bfloat16)
        .reshape(query_count, HD)
    )
    own_keyval = jnp.concatenate(
        [rotate(key_normed, cosine_table, sine_table), value_raw], axis=1
    ).astype(jnp.bfloat16)
    upper_queries = lax.dynamic_slice_in_dim(query_rows, upper_start, upper_span, 0)
    upper_order = lax.dynamic_slice_in_dim(query_order, upper_start, upper_span, 0)

    def group_forward(carried, key_rows, value_rows, key_order, least_block):

        def group_full_rows(inner):
            return tile_forward(inner, query_rows, query_order, key_rows, value_rows, key_order)

        def group_upper_rows(inner):
            part_state = tuple(
                (lax.dynamic_slice_in_dim(member, upper_start, upper_span, 0) for member in inner)
            )
            new_state = tile_forward(
                part_state, upper_queries, upper_order, key_rows, value_rows, key_order
            )
            return tuple(
                (
                    lax.dynamic_update_slice_in_dim(member, fresh, upper_start, 0)
                    for member, fresh in zip(inner, new_state)
                )
            )

        def group_no_rows(inner):
            return inner

        branch = jnp.where(
            least_block <= lower_block, 0, jnp.where(least_block <= upper_block, 1, 2)
        )
        return lax.switch(branch, [group_full_rows, group_upper_rows, group_no_rows], carried)

    group_blocks = 16
    group_count = num_blocks // group_blocks
    group_keys = group_blocks * BLK
    group_index = jnp.arange(group_count, dtype=jnp.int32)
    init_forward = (
        jnp.full((query_count,), -jnp.inf, jnp.float32),
        jnp.zeros((query_count,), jnp.float32),
        jnp.zeros((query_count, HD), jnp.float32),
    )
    all_keyval = lax.all_gather(
        own_keyval.reshape(2, BLK, 2 * HD), "ctx", axis=0, tiled=True
    )
    inverse = jnp.sum(
        jnp.where(block_map[None, :] == block_ids[:, None], block_ids[None, :], 0), axis=1
    )
    sorted_keyval = all_keyval[inverse].reshape(group_count, group_keys, 2 * HD)
    sorted_keys = sorted_keyval[:, :, :HD]
    sorted_values = sorted_keyval[:, :, HD:]

    def kept_forward(inner, scan_item):
        key_rows, value_rows, group_id = scan_item
        key_order = group_id * group_keys + jnp.arange(group_keys, dtype=jnp.int32)
        return (
            group_forward(inner, key_rows, value_rows, key_order, group_id * group_blocks),
            None,
        )

    forward_state, _ = lax.scan(
        kept_forward, init_forward, (sorted_keys, sorted_values, group_index)
    )
    row_peak, row_total, row_accum = forward_state
    log_total = row_peak + jnp.log(row_total)
    attn_rows = lax.optimization_barrier((row_accum / row_total[:, None]).astype(jnp.bfloat16))
    attn_flat = attn_rows.reshape(token_rows, HEADS * HD)
    branch_attn = jnp.dot(attn_flat, w_out, preferred_element_type=jnp.float32)
    after_attn = residual_in + rms_apply(branch_attn, gain_attn)
    normed_mid = rms_apply(after_attn, gain_ffn).astype(jnp.bfloat16)
    gate_up = jnp.dot(normed_mid, w_gateup, preferred_element_type=jnp.float32)
    gate_values = gate_up[:, :FF]
    up_values = gate_up[:, FF:]
    hidden = gated_unit(gate_values, up_values).astype(jnp.bfloat16)
    branch_ffn = jnp.dot(hidden, w_down, preferred_element_type=jnp.float32)
    result = after_attn + rms_apply(branch_ffn, gain_post)
    grad_branch, grad_gain_post = norm_back(branch_ffn, gain_post, grad_output)
    grad_branch_low = grad_branch.astype(jnp.bfloat16)
    grad_down = jnp.dot(hidden.T, grad_branch_low, preferred_element_type=jnp.float32)
    grad_hidden = jnp.dot(grad_branch_low, w_down.T, preferred_element_type=jnp.float32)
    _, unit_pull = jax.vjp(gated_unit, gate_values, up_values)
    grad_gate, grad_up = unit_pull(grad_hidden)
    grad_gateup_low = jnp.concatenate([grad_gate, grad_up], axis=1).astype(jnp.bfloat16)
    grad_gateup = jnp.dot(normed_mid.T, grad_gateup_low, preferred_element_type=jnp.float32)
    grad_normed_mid = jnp.dot(grad_gateup_low, w_gateup.T, preferred_element_type=jnp.float32)
    grad_mid_part, grad_gain_ffn = norm_back(after_attn, gain_ffn, grad_normed_mid)
    grad_after = grad_output + grad_mid_part
    grad_attn_branch, grad_gain_attn = norm_back(branch_attn, gain_attn, grad_after)
    grad_attn_low = grad_attn_branch.astype(jnp.bfloat16)
    grad_wout = jnp.dot(attn_flat.T, grad_attn_low, preferred_element_type=jnp.float32)
    grad_rows = lax.optimization_barrier(
        jnp.dot(grad_attn_low, w_out.T, preferred_element_type=jnp.float32).astype(jnp.bfloat16)
    ).reshape(query_count, HD)
    delta_rows = jnp.sum(grad_rows.astype(jnp.float32) * attn_rows.astype(jnp.float32), axis=1)
    upper_grads = lax.dynamic_slice_in_dim(grad_rows, upper_start, upper_span, 0)
    upper_lse = lax.dynamic_slice_in_dim(log_total, upper_start, upper_span, 0)
    upper_delta = lax.dynamic_slice_in_dim(delta_rows, upper_start, upper_span, 0)

    def tile_terms(grad_query, key_rows, value_rows, key_order, least_block):

        def tile_full_rows(inner):
            query_part, tile_rows = tile_backward(
                query_rows,
                query_order,
                grad_rows,
                log_total,
                delta_rows,
                key_rows,
                value_rows,
                key_order,
            )
            return (inner + query_part, tile_rows)

        def tile_upper_rows(inner):
            query_part, tile_rows = tile_backward(
                upper_queries,
                upper_order,
                upper_grads,
                upper_lse,
                upper_delta,
                key_rows,
                value_rows,
                key_order,
            )
            return (add_rows(inner, query_part, upper_start), tile_rows)

        def tile_no_rows(inner):
            return (inner, jnp.zeros((key_rows.shape[0], 2 * HD), jnp.float32))

        branch = jnp.where(
            least_block <= lower_block, 0, jnp.where(least_block <= upper_block, 1, 2)
        )
        return lax.switch(branch, [tile_full_rows, tile_upper_rows, tile_no_rows], grad_query)

    zero_query = jnp.zeros((query_count, HD), jnp.float32)

    def kept_backward(inner, scan_item):
        grad_query, term_rows = inner
        key_rows, value_rows, group_id = scan_item
        key_order = group_id * group_keys + jnp.arange(group_keys, dtype=jnp.int32)
        grad_query, tile_rows = tile_terms(
            grad_query, key_rows, value_rows, key_order, group_id * group_blocks
        )
        return ((grad_query, add_rows(term_rows, tile_rows, group_id * group_keys)), None)

    init_backward = (zero_query, jnp.zeros((num_blocks * BLK, 2 * HD), jnp.float32))
    backward_state, _ = lax.scan(
        kept_backward, init_backward, (sorted_keys, sorted_values, group_index)
    )
    grad_query_all, seq_terms = backward_state
    slot_terms = seq_terms.astype(jnp.bfloat16).reshape(num_blocks, BLK, 2 * HD)[block_map]
    key_terms = lax.psum_scatter(slot_terms, "ctx", scatter_dimension=0, tiled=True).reshape(
        token_rows, 2 * HD
    ).astype(jnp.float32)
    grad_key_rot = key_terms[:, :HD]
    grad_value = key_terms[:, HD:]
    grad_query_rot = grad_query_all.reshape(token_rows, HEADS, HD)
    grad_query_normed = rotate_back(
        grad_query_rot * query_scale, cosine_table[:, None], sine_table[:, None]
    )
    grad_query_raw, grad_gain_query = norm_back(query_raw, gain_query, grad_query_normed)
    grad_key_normed = rotate_back(grad_key_rot, cosine_table, sine_table)
    grad_key_raw, grad_gain_key = norm_back(key_raw, gain_key, grad_key_normed)
    grad_projected = jnp.concatenate(
        [grad_query_raw.reshape(token_rows, HEADS * HD), grad_key_raw, grad_value], axis=1
    ).astype(jnp.bfloat16)
    grad_wqkv = jnp.dot(normed_in.T, grad_projected, preferred_element_type=jnp.float32)
    grad_normed_in = jnp.dot(grad_projected, w_qkv.T, preferred_element_type=jnp.float32)
    grad_in_part, grad_gain_in = norm_back(residual_in, gain_in, grad_normed_in)
    grad_input = grad_after + grad_in_part
    local_matrix = jnp.concatenate(
        [
            grad_wqkv.reshape(-1),
            grad_wout.reshape(-1),
            grad_gateup.reshape(-1),
            grad_down.reshape(-1),
        ]
    )
    local_gain = jnp.concatenate(
        [
            grad_gain_in,
            grad_gain_query,
            grad_gain_key,
            grad_gain_attn,
            grad_gain_ffn,
            grad_gain_post,
        ]
    )
    device_count = gathered.shape[0] // matrices.shape[0]
    matrix_grad = (
        lax.psum_scatter(
            local_matrix.astype(jnp.bfloat16).reshape(device_count, -1, LANES),
            ("ctx", "fsdp"),
            scatter_dimension=0,
            tiled=True,
        )
        .reshape(-1)
        .astype(jnp.float32)
    )
    gain_grad = lax.psum_scatter(local_gain, ("ctx", "fsdp"), scatter_dimension=0, tiled=True)
    new_matrices, new_first, new_second = adamw_update(
        matrices, first_moment, second_moment, matrix_grad
    )
    new_gains, new_gain_first, new_gain_second = adamw_update(
        gain_offsets, gain_first, gain_second, gain_grad
    )
    return (
        result[None],
        grad_input[None],
        matrix_grad,
        gain_grad,
        new_matrices,
        new_gains,
        new_first,
        new_second,
        new_gain_first,
        new_gain_second,
    )


def solution(mesh):
    return jax.shard_map(
        shards,
        mesh=mesh,
        in_specs=(
            P("fsdp", "ctx", None),
            P("fsdp", "ctx", None),
            P("fsdp", "ctx"),
            P(),
            P(("ctx", "fsdp")),
            P(("ctx", "fsdp")),
            P(("ctx", "fsdp")),
            P(("ctx", "fsdp")),
            P(("ctx", "fsdp")),
            P(("ctx", "fsdp")),
        ),
        out_specs=(
            P("fsdp", "ctx", None),
            P("fsdp", "ctx", None),
            P(("ctx", "fsdp")),
            P(("ctx", "fsdp")),
            P(("ctx", "fsdp")),
            P(("ctx", "fsdp")),
            P(("ctx", "fsdp")),
            P(("ctx", "fsdp")),
            P(("ctx", "fsdp")),
            P(("ctx", "fsdp")),
        ),
        check_vma=False,
    )
```

```python
import functools

import jax
import jax.numpy as jnp
from jax import lax
from jax.experimental import pallas as pl
from jax.experimental.pallas import tpu as pltpu
from jax.sharding import PartitionSpec as P

D = 640
HEADS = 4
HD = 256
FF = 2048
BLK = 64
STEP = 3


NORM_EPS = 1e-06
ROPE_BASE = 1000000.0
LEARN_RATE = 0.03
BETA_ONE = 0.9
BETA_TWO = 0.95
ADAM_EPS = 1e-08
DECAY_RATE = 0.1

LANES = 128
ROW_TILE = 16


def bit_of(index, bit):
    return lax.rem(index // (1 << bit), 2)


def flipped(index, bit):
    return index + (1 - 2 * bit_of(index, bit)) * (1 << bit)


def compress(index, bits):
    slot = 0
    for rank, bit in enumerate(bits):
        slot = slot + bit_of(index, bit) * (1 << rank)
    return slot


class Group:
    def __init__(self, ctx_size, fsdp_size, whole):
        self.fsdp_size = fsdp_size
        self.whole = whole
        self.size = ctx_size * fsdp_size if whole else ctx_size
        self.bits = self.size.bit_length() - 1

    def position(self):
        if self.whole:
            return lax.axis_index("ctx") * self.fsdp_size + lax.axis_index("fsdp")
        return lax.axis_index("ctx")

    def place(self, index):
        if self.whole:
            return (index // self.fsdp_size, lax.rem(index, self.fsdp_size))
        return (index, lax.axis_index("fsdp"))

    def orders(self):
        if self.whole:
            upper = list(range(3, self.bits))
            return ([1, 2, 0] + upper, [1, 0] + upper + [2])
        upper = list(range(2, self.bits))
        return ([0, 1] + upper, [0] + upper + [1])


def row_parts(rows, share=9):
    middle = max(1, rows * share // 16 // ROW_TILE) * ROW_TILE
    return ((0, middle), (middle, rows - middle))


def enter(group, me):
    barrier = pltpu.get_barrier_semaphore()
    for bit in range(group.bits):
        pl.semaphore_signal(
            barrier,
            inc=1,
            device_id=group.place(flipped(me, bit)),
            device_id_type=pl.DeviceIdType.MESH,
        )
    pl.semaphore_wait(barrier, group.bits)


def gather_kernel(group, parts, array_count, *refs):
    own_refs = refs[:array_count]
    out_refs = refs[array_count : 2 * array_count]
    local_sem, send_sem, recv_sem = refs[2 * array_count :]
    me = group.position()
    enter(group, me)
    orders = [part[3][::-1] for part in parts]
    locals_ = []
    for number in range(array_count):
        copy = pltpu.make_async_copy(
            own_refs[number], out_refs[number].at[me], local_sem.at[number]
        )
        copy.start()
        locals_.append(copy)

    def transfer(part, block, step, own=False):
        number, first, count, _ = parts[part]
        rows = pl.ds(first, count)
        target = out_refs[number].at[block, rows]
        return pltpu.make_async_remote_copy(
            src_ref=own_refs[number].at[rows] if own else target,
            dst_ref=target,
            send_sem=send_sem.at[part, (1 << step) + compress(block, orders[part][:step])],
            recv_sem=recv_sem.at[part, block],
            device_id=group.place(flipped(me, orders[part][step])),
            device_id_type=pl.DeviceIdType.MESH,
        )

    def block_at(part, step, count):
        block = flipped(me, orders[part][step])
        for rank in range(step):
            bit = orders[part][rank]
            block = block + bit_of(count, rank) * (1 - 2 * bit_of(me, bit)) * (1 << bit)
        return block

    for step in range(group.bits):
        for part in range(len(parts)):
            transfer(part, me, step, True).start()
    for step in range(group.bits):

        def arrived(count, carried, step=step):
            for part in range(len(parts)):
                block = block_at(part, step, count)
                transfer(part, block, step).wait_recv()
                for later in range(step + 1, group.bits):
                    transfer(part, block, later).start()
            return carried

        lax.fori_loop(0, 1 << step, arrived, 0)
    for copy in locals_:
        copy.wait()
    for step in range(group.bits):
        for part in range(len(parts)):
            transfer(part, me, step, True).wait_send()
    for step in range(group.bits - 1):

        def sent(count, carried, step=step):
            for part in range(len(parts)):
                block = block_at(part, step, count)
                for later in range(step + 1, group.bits):
                    transfer(part, block, later).wait_send()
            return carried

        lax.fori_loop(0, 1 << step, sent, 0)


def gather_all(group, parts, owns, collective_id):
    any_spec = pl.BlockSpec(memory_space=pl.ANY)
    return pl.pallas_call(
        functools.partial(gather_kernel, group, parts, len(owns)),
        out_shape=[jax.ShapeDtypeStruct((group.size,) + own.shape, own.dtype) for own in owns],
        in_specs=[any_spec] * len(owns),
        out_specs=[any_spec] * len(owns),
        scratch_shapes=[
            pltpu.SemaphoreType.DMA((len(owns),)),
            pltpu.SemaphoreType.DMA((len(parts), group.size)),
            pltpu.SemaphoreType.DMA((len(parts), group.size)),
        ],
        compiler_params=pltpu.CompilerParams(
            collective_id=collective_id, has_side_effects=True
        ),
    )(*owns)


def reduce_kernel(group, parts, piece_rows, array_count, *refs):
    piece_count = sum(len(rows) for rows in piece_rows)
    piece_refs = refs[:piece_count]
    out_refs = refs[piece_count : piece_count + array_count]
    refs = refs[piece_count + array_count :]
    term_refs, refs = refs[:array_count], refs[array_count:]
    held = [
        refs[part * group.bits : (part + 1) * group.bits] for part in range(len(parts))
    ]
    local_sem, send_sem, recv_sem = refs[len(parts) * group.bits :]
    me = group.position()
    copies = []
    for number in range(array_count):
        first = 0
        for rows in piece_rows[number]:
            copy = pltpu.make_async_copy(
                piece_refs[len(copies)],
                term_refs[number].at[pl.ds(first, rows)],
                local_sem.at[len(copies)],
            )
            copy.start()
            copies.append(copy)
            first += rows
    enter(group, me)
    for copy in copies:
        copy.wait()
    orders = [part[3] for part in parts]

    def source_of(part, step, block):
        number, first, count, _ = parts[part]
        if step == 0:
            each = term_refs[number].shape[0] // group.size
            start = pl.multiple_of(block * each + first, first_tile(first, each))
            return term_refs[number].at[pl.ds(start, count)]
        return held[part][step - 1].at[compress(block, orders[part][step:])]

    def transfer(part, step, block):
        slot = compress(block, orders[part][step + 1 :])
        return pltpu.make_async_remote_copy(
            src_ref=source_of(part, step, block),
            dst_ref=held[part][step].at[slot],
            send_sem=send_sem.at[part, block_count(step) + slot],
            recv_sem=recv_sem.at[part, block_count(step) + slot],
            device_id=group.place(flipped(me, orders[part][step])),
            device_id_type=pl.DeviceIdType.MESH,
        )

    def block_at(part, step, count, away):
        order = orders[part]
        block = flipped(me, order[step]) if away else me
        left = order[step + 1 :]
        for rank, bit in enumerate(left):
            chosen = bit_of(count, len(left) - 1 - rank)
            block = block + chosen * (1 - 2 * bit_of(me, bit)) * (1 << bit)
        return block

    def block_count(step):
        return 1 << (group.bits - 1 - step)

    def first_sends(index, carried):
        for part in range(len(parts)):
            transfer(part, 0, block_at(part, 0, block_count(0) - 1 - index, True)).start()
        return carried

    lax.fori_loop(0, block_count(0), first_sends, 0)
    for step in range(group.bits):
        total = block_count(step)
        last = step == group.bits - 1

        def arrived(index, carried, step=step, total=total, last=last, onward=True):
            for part in range(len(parts)):
                number, first, count, _ = parts[part]
                block = block_at(part, step, total - 1 - index, False)
                transfer(part, step, block).wait_recv()
                slot = compress(block, orders[part][step + 1 :])
                mine = source_of(part, step, block)[...].astype(jnp.float32)
                summed = held[part][step][slot].astype(jnp.float32) + mine
                if last:
                    out_refs[number][pl.ds(first, count), :] = summed
                else:
                    held[part][step][slot] = summed.astype(held[part][step].dtype)
                    if onward:
                        transfer(part, step + 1, block).start()
            return carried

        if last:
            arrived(0, 0)
        else:
            lax.fori_loop(0, total // 2, arrived, 0)
            lax.fori_loop(total // 2, total, functools.partial(arrived, onward=False), 0)
    for step in range(group.bits):

        def sent(count, carried, step=step):
            for part in range(len(parts)):
                transfer(part, step, block_at(part, step, count, True)).wait_send()
            return carried

        lax.fori_loop(0, block_count(step), sent, 0)


def first_tile(first, each):
    tile = ROW_TILE
    while first % tile or each % tile:
        tile //= 2
    return tile


def reduce_all(group, parts, pieces, collective_id):
    flat = [piece for array in pieces for piece in array]
    rows = [sum(piece.shape[0] for piece in array) for array in pieces]
    widths = [array[0].shape[1] for array in pieces]
    types = [array[0].dtype for array in pieces]
    return pl.pallas_call(
        functools.partial(
            reduce_kernel,
            group,
            parts,
            [[piece.shape[0] for piece in array] for array in pieces],
            len(pieces),
        ),
        out_shape=[
            jax.ShapeDtypeStruct((total // group.size, width), jnp.float32)
            for total, width in zip(rows, widths)
        ],
        in_specs=[pl.BlockSpec(memory_space=pl.ANY)] * len(flat),
        out_specs=[pl.BlockSpec(memory_space=pltpu.VMEM)] * len(pieces),
        scratch_shapes=[
            pltpu.VMEM((total, width), kind) for total, width, kind in zip(rows, widths, types)
        ]
        + [
            pltpu.VMEM((1 << (group.bits - 1 - step), count, widths[number]), types[number])
            for number, _, count, _ in parts
            for step in range(group.bits)
        ]
        + [
            pltpu.SemaphoreType.DMA((len(flat),)),
            pltpu.SemaphoreType.DMA((len(parts), group.size)),
            pltpu.SemaphoreType.DMA((len(parts), group.size)),
        ],
        compiler_params=pltpu.CompilerParams(
            collective_id=collective_id, has_side_effects=True, vmem_limit_bytes=56 << 20
        ),
    )(*flat)


def rms_apply(values, offset):
    scale_rows = lax.rsqrt(jnp.mean(values * values, axis=-1, keepdims=True) + NORM_EPS)
    return values * scale_rows * (1.0 + offset)


def norm_back(values, offset, upstream):
    _, pullback = jax.vjp(rms_apply, values, offset)
    return pullback(upstream)


def gated_unit(gate_values, up_values):
    return jax.nn.gelu(gate_values, approximate=True) * up_values


def rope_tables(token_pos):
    half_width = HD // 2
    exponents = jnp.arange(half_width, dtype=jnp.float32) * (2.0 / HD)
    frequency = jnp.power(jnp.float32(ROPE_BASE), -exponents)
    angles = token_pos.astype(jnp.float32)[:, None] * frequency[None, :]
    cosine_table = jnp.cos(angles)
    sine_table = jnp.sin(angles)
    return (
        jnp.concatenate([cosine_table, cosine_table], axis=-1),
        jnp.concatenate([sine_table, sine_table], axis=-1),
    )


def rotate(values, cosine_table, sine_table):
    half_width = values.shape[-1] // 2
    first_half = values[..., :half_width]
    second_half = values[..., half_width:]
    turned = jnp.concatenate([-second_half, first_half], axis=-1)
    return values * cosine_table + turned * sine_table


def rotate_back(upstream, cosine_table, sine_table):
    half_width = upstream.shape[-1] // 2
    weighted = upstream * sine_table
    turned = jnp.concatenate([weighted[..., half_width:], -weighted[..., :half_width]], axis=-1)
    return upstream * cosine_table + turned


def split_weights(flat_values):
    width_qkv = HEADS * HD + 2 * HD
    first_end = D * width_qkv
    second_end = first_end + HEADS * HD * D
    third_end = second_end + 2 * D * FF
    return (
        flat_values[:first_end].reshape(D, width_qkv),
        flat_values[first_end:second_end].reshape(HEADS * HD, D),
        flat_values[second_end:third_end].reshape(D, 2 * FF),
        flat_values[third_end:].reshape(FF, D),
    )


def split_gains(flat_values):
    return (
        flat_values[:D],
        flat_values[D : D + HD],
        flat_values[D + HD : D + 2 * HD],
        flat_values[D + 2 * HD : 2 * D + 2 * HD],
        flat_values[2 * D + 2 * HD : 3 * D + 2 * HD],
        flat_values[3 * D + 2 * HD :],
    )


def adamw_update(weights, first_state, second_state, gradient):
    new_first = BETA_ONE * first_state + (1.0 - BETA_ONE) * gradient
    new_second = BETA_TWO * second_state + (1.0 - BETA_TWO) * gradient * gradient
    first_hat = new_first / (1.0 - BETA_ONE**STEP)
    second_hat = new_second / (1.0 - BETA_TWO**STEP)
    update = first_hat / (jnp.sqrt(second_hat) + ADAM_EPS) + DECAY_RATE * weights
    return (weights - LEARN_RATE * update, new_first, new_second)


def tile_forward(carried, query_rows, query_order, key_rows, value_rows, key_order):
    row_peak, row_total, row_accum = carried
    scores = lax.dot_general(
        key_rows, query_rows, (((1,), (1,)), ((), ())), preferred_element_type=jnp.float32
    )
    allowed = key_order[:, None] <= query_order[None, :]
    masked = jnp.where(allowed, scores, -jnp.inf)
    new_peak = jnp.maximum(row_peak, jnp.max(masked, axis=0))
    weights = jnp.exp(masked - new_peak[None, :])
    rescale = jnp.exp(row_peak - new_peak)
    new_total = row_total * rescale + jnp.sum(weights, axis=0)
    weights_low = weights.astype(jnp.bfloat16)
    update = lax.dot_general(
        weights_low, value_rows, (((0,), (0,)), ((), ())), preferred_element_type=jnp.float32
    )
    return (new_peak, new_total, row_accum * rescale[:, None] + update)


def tile_backward(
    query_rows, query_order, grad_rows, log_total, delta_rows, key_rows, value_rows, key_order
):
    scores = lax.dot_general(
        key_rows, query_rows, (((1,), (1,)), ((), ())), preferred_element_type=jnp.float32
    )
    allowed = key_order[:, None] <= query_order[None, :]
    probability = jnp.where(allowed, jnp.exp(scores - log_total[None, :]), 0.0)
    probability_low = probability.astype(jnp.bfloat16)
    value_part = jnp.dot(probability_low, grad_rows, preferred_element_type=jnp.float32)
    grad_prob = lax.dot_general(
        value_rows, grad_rows, (((1,), (1,)), ((), ())), preferred_element_type=jnp.float32
    )
    grad_scores = (probability * (grad_prob - delta_rows[None, :])).astype(jnp.bfloat16)
    query_part = lax.dot_general(
        grad_scores, key_rows, (((0,), (0,)), ((), ())), preferred_element_type=jnp.float32
    )
    key_part = jnp.dot(grad_scores, query_rows, preferred_element_type=jnp.float32)
    return (query_part, jnp.concatenate([key_part, value_part], axis=1))


def add_rows(term_rows, tile_rows, first_row):
    current = lax.dynamic_slice_in_dim(term_rows, first_row, tile_rows.shape[0], 0)
    return lax.dynamic_update_slice_in_dim(term_rows, current + tile_rows, first_row, 0)


def shards(
    inputs,
    cotangent,
    positions,
    block_map,
    matrices,
    gain_offsets,
    first_moment,
    second_moment,
    gain_first,
    gain_second,
):
    fsdp_size = lax.axis_size("fsdp")
    every = Group(lax.axis_size("ctx"), fsdp_size, True)
    sequence = Group(lax.axis_size("ctx"), fsdp_size, False)
    shard_rows = matrices.shape[0] // LANES
    padded_rows = -(-shard_rows // ROW_TILE) * ROW_TILE
    extra_rows = padded_rows - shard_rows
    (early, late), (order_a, order_b) = row_parts(padded_rows), every.orders()
    shard_parts = ((0,) + early + (order_a,), (0,) + late + (order_b,))
    gain_count = gain_offsets.shape[0]
    own_gains = jnp.pad(
        gain_offsets.astype(jnp.bfloat16).reshape(1, gain_count),
        ((0, ROW_TILE - 1), (0, LANES - gain_count)),
    )
    gathered, gain_rows = gather_all(
        every,
        shard_parts + ((1, 0, ROW_TILE, order_a),),
        [
            jnp.pad(
                matrices.astype(jnp.bfloat16).reshape(shard_rows, LANES), ((0, extra_rows), (0, 0))
            ),
            own_gains,
        ],
        0,
    )
    gathered = gathered[:, :shard_rows].reshape(-1)
    gains_low = gain_rows[:, 0, :gain_count].reshape(-1)
    w_qkv, w_out, w_gateup, w_down = split_weights(gathered)
    gain_in, gain_query, gain_key, gain_attn, gain_ffn, gain_post = split_gains(
        gains_low.astype(jnp.float32)
    )
    token_rows = inputs.shape[1]
    query_count = token_rows * HEADS
    upper_span = BLK * HEADS
    query_scale = HD ** (-0.5)
    residual_in = inputs[0]
    grad_output = cotangent[0]
    num_blocks = block_map.shape[0]
    block_ids = jnp.arange(num_blocks, dtype=jnp.int32)
    block_offsets = jnp.arange(BLK, dtype=jnp.int32)
    ctx_index = lax.axis_index("ctx")
    own_blocks = jnp.sum(
        jnp.where(
            (2 * ctx_index + jnp.arange(2, dtype=jnp.int32))[:, None] == block_ids[None, :],
            block_map[None, :],
            0,
        ),
        axis=1,
    )
    lower_block = jnp.min(own_blocks)
    upper_block = jnp.max(own_blocks)
    upper_start = jnp.where(own_blocks[1] > own_blocks[0], 1, 0) * upper_span
    token_order = (own_blocks[:, None] * BLK + block_offsets[None, :]).reshape(token_rows)
    query_order = jnp.repeat(token_order, HEADS)
    cosine_table, sine_table = rope_tables(positions[0])
    normed_in = rms_apply(residual_in, gain_in).astype(jnp.bfloat16)
    projected = jnp.dot(normed_in, w_qkv, preferred_element_type=jnp.float32)
    query_raw = projected[:, : HEADS * HD].reshape(token_rows, HEADS, HD)
    key_raw = projected[:, HEADS * HD : HEADS * HD + HD]
    value_raw = projected[:, HEADS * HD + HD :]
    query_normed = rms_apply(query_raw, gain_query)
    key_normed = rms_apply(key_raw, gain_key)
    query_rows = (
        (rotate(query_normed, cosine_table[:, None], sine_table[:, None]) * query_scale)
        .astype(jnp.bfloat16)
        .reshape(query_count, HD)
    )
    own_keyval = jnp.concatenate(
        [rotate(key_normed, cosine_table, sine_table), value_raw], axis=1
    ).astype(jnp.bfloat16)
    upper_queries = lax.dynamic_slice_in_dim(query_rows, upper_start, upper_span, 0)
    upper_order = lax.dynamic_slice_in_dim(query_order, upper_start, upper_span, 0)

    def group_forward(carried, key_rows, value_rows, key_order, least_block):

        def group_full_rows(inner):
            return tile_forward(inner, query_rows, query_order, key_rows, value_rows, key_order)

        def group_upper_rows(inner):
            part_state = tuple(
                (lax.dynamic_slice_in_dim(member, upper_start, upper_span, 0) for member in inner)
            )
            new_state = tile_forward(
                part_state, upper_queries, upper_order, key_rows, value_rows, key_order
            )
            return tuple(
                (
                    lax.dynamic_update_slice_in_dim(member, fresh, upper_start, 0)
                    for member, fresh in zip(inner, new_state)
                )
            )

        def group_no_rows(inner):
            return inner

        branch = jnp.where(
            least_block <= lower_block, 0, jnp.where(least_block <= upper_block, 1, 2)
        )
        return lax.switch(branch, [group_full_rows, group_upper_rows, group_no_rows], carried)

    group_blocks = 16
    group_count = num_blocks // group_blocks
    group_keys = group_blocks * BLK
    group_index = jnp.arange(group_count, dtype=jnp.int32)
    init_forward = (
        jnp.full((query_count,), -jnp.inf, jnp.float32),
        jnp.zeros((query_count,), jnp.float32),
        jnp.zeros((query_count, HD), jnp.float32),
    )
    (early_kv, late_kv), (order_c, order_d) = row_parts(token_rows, 8), sequence.orders()
    keyval_parts = ((0,) + early_kv + (order_c,), (0,) + late_kv + (order_d,))
    (all_keyval,) = gather_all(sequence, keyval_parts, [own_keyval], 2)
    all_keyval = all_keyval.reshape(num_blocks, BLK, 2 * HD)
    inverse = jnp.sum(
        jnp.where(block_map[None, :] == block_ids[:, None], block_ids[None, :], 0), axis=1
    )
    sorted_keyval = all_keyval[inverse].reshape(group_count, group_keys, 2 * HD)
    sorted_keys = sorted_keyval[:, :, :HD]
    sorted_values = sorted_keyval[:, :, HD:]

    def kept_forward(inner, scan_item):
        key_rows, value_rows, group_id = scan_item
        key_order = group_id * group_keys + jnp.arange(group_keys, dtype=jnp.int32)
        return (
            group_forward(inner, key_rows, value_rows, key_order, group_id * group_blocks),
            None,
        )

    forward_state, _ = lax.scan(
        kept_forward, init_forward, (sorted_keys, sorted_values, group_index)
    )
    row_peak, row_total, row_accum = forward_state
    log_total = row_peak + jnp.log(row_total)
    attn_rows = lax.optimization_barrier((row_accum / row_total[:, None]).astype(jnp.bfloat16))
    attn_flat = attn_rows.reshape(token_rows, HEADS * HD)
    branch_attn = jnp.dot(attn_flat, w_out, preferred_element_type=jnp.float32)
    after_attn = residual_in + rms_apply(branch_attn, gain_attn)
    normed_mid = rms_apply(after_attn, gain_ffn).astype(jnp.bfloat16)
    gate_up = jnp.dot(normed_mid, w_gateup, preferred_element_type=jnp.float32)
    gate_values = gate_up[:, :FF]
    up_values = gate_up[:, FF:]
    hidden = gated_unit(gate_values, up_values).astype(jnp.bfloat16)
    branch_ffn = jnp.dot(hidden, w_down, preferred_element_type=jnp.float32)
    result = after_attn + rms_apply(branch_ffn, gain_post)
    grad_branch, grad_gain_post = norm_back(branch_ffn, gain_post, grad_output)
    grad_branch_low = grad_branch.astype(jnp.bfloat16)
    grad_down = jnp.dot(hidden.T, grad_branch_low, preferred_element_type=jnp.float32)
    grad_hidden = jnp.dot(grad_branch_low, w_down.T, preferred_element_type=jnp.float32)
    _, unit_pull = jax.vjp(gated_unit, gate_values, up_values)
    grad_gate, grad_up = unit_pull(grad_hidden)
    grad_gateup_low = jnp.concatenate([grad_gate, grad_up], axis=1).astype(jnp.bfloat16)
    grad_gateup = jnp.dot(normed_mid.T, grad_gateup_low, preferred_element_type=jnp.float32)
    grad_normed_mid = jnp.dot(grad_gateup_low, w_gateup.T, preferred_element_type=jnp.float32)
    grad_mid_part, grad_gain_ffn = norm_back(after_attn, gain_ffn, grad_normed_mid)
    grad_after = grad_output + grad_mid_part
    grad_attn_branch, grad_gain_attn = norm_back(branch_attn, gain_attn, grad_after)
    grad_attn_low = grad_attn_branch.astype(jnp.bfloat16)
    grad_wout = jnp.dot(attn_flat.T, grad_attn_low, preferred_element_type=jnp.float32)
    grad_rows = lax.optimization_barrier(
        jnp.dot(grad_attn_low, w_out.T, preferred_element_type=jnp.float32).astype(jnp.bfloat16)
    ).reshape(query_count, HD)
    delta_rows = jnp.sum(grad_rows.astype(jnp.float32) * attn_rows.astype(jnp.float32), axis=1)
    upper_grads = lax.dynamic_slice_in_dim(grad_rows, upper_start, upper_span, 0)
    upper_lse = lax.dynamic_slice_in_dim(log_total, upper_start, upper_span, 0)
    upper_delta = lax.dynamic_slice_in_dim(delta_rows, upper_start, upper_span, 0)

    def tile_terms(grad_query, key_rows, value_rows, key_order, least_block):

        def tile_full_rows(inner):
            query_part, tile_rows = tile_backward(
                query_rows,
                query_order,
                grad_rows,
                log_total,
                delta_rows,
                key_rows,
                value_rows,
                key_order,
            )
            return (inner + query_part, tile_rows)

        def tile_upper_rows(inner):
            query_part, tile_rows = tile_backward(
                upper_queries,
                upper_order,
                upper_grads,
                upper_lse,
                upper_delta,
                key_rows,
                value_rows,
                key_order,
            )
            return (add_rows(inner, query_part, upper_start), tile_rows)

        def tile_no_rows(inner):
            return (inner, jnp.zeros((key_rows.shape[0], 2 * HD), jnp.float32))

        branch = jnp.where(
            least_block <= lower_block, 0, jnp.where(least_block <= upper_block, 1, 2)
        )
        return lax.switch(branch, [tile_full_rows, tile_upper_rows, tile_no_rows], grad_query)

    zero_query = jnp.zeros((query_count, HD), jnp.float32)

    def kept_backward(inner, scan_item):
        grad_query, term_rows = inner
        key_rows, value_rows, group_id = scan_item
        key_order = group_id * group_keys + jnp.arange(group_keys, dtype=jnp.int32)
        grad_query, tile_rows = tile_terms(
            grad_query, key_rows, value_rows, key_order, group_id * group_blocks
        )
        return ((grad_query, add_rows(term_rows, tile_rows, group_id * group_keys)), None)

    init_backward = (zero_query, jnp.zeros((num_blocks * BLK, 2 * HD), jnp.float32))
    backward_state, _ = lax.scan(
        kept_backward, init_backward, (sorted_keys, sorted_values, group_index)
    )
    grad_query_all, seq_terms = backward_state
    slot_terms = seq_terms.astype(jnp.bfloat16).reshape(num_blocks, BLK, 2 * HD)[block_map]
    (key_terms,) = reduce_all(
        sequence, keyval_parts, [[slot_terms.reshape(num_blocks * BLK, 2 * HD)]], 3
    )
    grad_key_rot = key_terms[:, :HD]
    grad_value = key_terms[:, HD:]
    grad_query_rot = grad_query_all.reshape(token_rows, HEADS, HD)
    grad_query_normed = rotate_back(
        grad_query_rot * query_scale, cosine_table[:, None], sine_table[:, None]
    )
    grad_query_raw, grad_gain_query = norm_back(query_raw, gain_query, grad_query_normed)
    grad_key_normed = rotate_back(grad_key_rot, cosine_table, sine_table)
    grad_key_raw, grad_gain_key = norm_back(key_raw, gain_key, grad_key_normed)
    grad_projected = jnp.concatenate(
        [grad_query_raw.reshape(token_rows, HEADS * HD), grad_key_raw, grad_value], axis=1
    ).astype(jnp.bfloat16)
    grad_wqkv = jnp.dot(normed_in.T, grad_projected, preferred_element_type=jnp.float32)
    grad_normed_in = jnp.dot(grad_projected, w_qkv.T, preferred_element_type=jnp.float32)
    grad_in_part, grad_gain_in = norm_back(residual_in, gain_in, grad_normed_in)
    grad_input = grad_after + grad_in_part
    local_gain = jnp.concatenate(
        [
            grad_gain_in,
            grad_gain_query,
            grad_gain_key,
            grad_gain_attn,
            grad_gain_ffn,
            grad_gain_post,
        ]
    )
    gain_terms = jnp.pad(
        local_gain.reshape(every.size, 1, gain_count), ((0, 0), (0, 7), (0, LANES - gain_count))
    ).reshape(every.size * 8, LANES)
    matrix_terms = [
        term.astype(jnp.bfloat16).reshape(-1, LANES)
        for term in (grad_wqkv, grad_wout, grad_gateup, grad_down)
    ]
    if extra_rows:
        whole_terms = jnp.concatenate(matrix_terms).reshape(every.size, shard_rows, LANES)
        matrix_terms = [
            jnp.pad(whole_terms, ((0, 0), (0, extra_rows), (0, 0))).reshape(-1, LANES)
        ]
    matrix_rows, gain_sums = reduce_all(
        every, shard_parts + ((1, 0, 8, order_a),), [matrix_terms, [gain_terms]], 1
    )
    matrix_grad = matrix_rows[:shard_rows].reshape(-1)
    gain_grad = gain_sums[0, :gain_count]
    new_matrices, new_first, new_second = adamw_update(
        matrices, first_moment, second_moment, matrix_grad
    )
    new_gains, new_gain_first, new_gain_second = adamw_update(
        gain_offsets, gain_first, gain_second, gain_grad
    )
    return (
        result[None],
        grad_input[None],
        matrix_grad,
        gain_grad,
        new_matrices,
        new_gains,
        new_first,
        new_second,
        new_gain_first,
        new_gain_second,
    )


def solution(mesh):
    return jax.shard_map(
        shards,
        mesh=mesh,
        in_specs=(
            P("fsdp", "ctx", None),
            P("fsdp", "ctx", None),
            P("fsdp", "ctx"),
            P(),
            P(("ctx", "fsdp")),
            P(("ctx", "fsdp")),
            P(("ctx", "fsdp")),
            P(("ctx", "fsdp")),
            P(("ctx", "fsdp")),
            P(("ctx", "fsdp")),
        ),
        out_specs=(
            P("fsdp", "ctx", None),
            P("fsdp", "ctx", None),
            P(("ctx", "fsdp")),
            P(("ctx", "fsdp")),
            P(("ctx", "fsdp")),
            P(("ctx", "fsdp")),
            P(("ctx", "fsdp")),
            P(("ctx", "fsdp")),
            P(("ctx", "fsdp")),
            P(("ctx", "fsdp")),
        ),
        check_vma=False,
    )
```

```python
import functools

import jax
import jax.numpy as jnp
from jax import lax
from jax.experimental import pallas as pl
from jax.experimental.pallas import tpu as pltpu
from jax.sharding import PartitionSpec as P

D = 640
HEADS = 4
HD = 256
FF = 2048
BLK = 64
STEP = 3


NORM_EPS = 1e-06
ROPE_BASE = 1000000.0
LEARN_RATE = 0.03
BETA_ONE = 0.9
BETA_TWO = 0.95
ADAM_EPS = 1e-08
DECAY_RATE = 0.1

LANES = 128
ROW_TILE = 16


def bit_of(index, bit):
    return lax.rem(index // (1 << bit), 2)


def flipped(index, bit):
    return index + (1 - 2 * bit_of(index, bit)) * (1 << bit)


def compress(index, bits):
    slot = 0
    for rank, bit in enumerate(bits):
        slot = slot + bit_of(index, bit) * (1 << rank)
    return slot


class Group:
    def __init__(self, ctx_size, fsdp_size, whole):
        self.fsdp_size = fsdp_size
        self.whole = whole
        self.size = ctx_size * fsdp_size if whole else ctx_size
        self.bits = self.size.bit_length() - 1

    def position(self):
        if self.whole:
            return lax.axis_index("ctx") * self.fsdp_size + lax.axis_index("fsdp")
        return lax.axis_index("ctx")

    def place(self, index):
        if self.whole:
            return (index // self.fsdp_size, lax.rem(index, self.fsdp_size))
        return (index, lax.axis_index("fsdp"))

    def orders(self):
        if self.whole:
            upper = list(range(3, self.bits))
            return ([1, 2, 0] + upper, [1, 0] + upper + [2])
        upper = list(range(2, self.bits))
        return ([0, 1] + upper, [0] + upper + [1])


def row_parts(rows, share=9):
    middle = max(1, rows * share // 16 // ROW_TILE) * ROW_TILE
    return ((0, middle), (middle, rows - middle))


def enter(group, me):
    barrier = pltpu.get_barrier_semaphore()
    for bit in range(group.bits):
        pl.semaphore_signal(
            barrier,
            inc=1,
            device_id=group.place(flipped(me, bit)),
            device_id_type=pl.DeviceIdType.MESH,
        )
    pl.semaphore_wait(barrier, group.bits)


def gather_kernel(group, parts, array_count, *refs):
    own_refs = refs[:array_count]
    out_refs = refs[array_count : 2 * array_count]
    local_sem, send_sem, recv_sem = refs[2 * array_count :]
    me = group.position()
    enter(group, me)
    orders = [part[3][::-1] for part in parts]
    locals_ = []
    for number in range(array_count):
        copy = pltpu.make_async_copy(
            own_refs[number], out_refs[number].at[me], local_sem.at[number]
        )
        copy.start()
        locals_.append(copy)

    def transfer(part, block, step, own=False):
        number, first, count, _ = parts[part]
        rows = pl.ds(first, count)
        target = out_refs[number].at[block, rows]
        return pltpu.make_async_remote_copy(
            src_ref=own_refs[number].at[rows] if own else target,
            dst_ref=target,
            send_sem=send_sem.at[part, (1 << step) + compress(block, orders[part][:step])],
            recv_sem=recv_sem.at[part, block],
            device_id=group.place(flipped(me, orders[part][step])),
            device_id_type=pl.DeviceIdType.MESH,
        )

    def block_at(part, step, count):
        block = flipped(me, orders[part][step])
        for rank in range(step):
            bit = orders[part][rank]
            block = block + bit_of(count, rank) * (1 - 2 * bit_of(me, bit)) * (1 << bit)
        return block

    for step in range(group.bits):
        for part in range(len(parts)):
            transfer(part, me, step, True).start()
    for step in range(group.bits):

        def arrived(count, carried, step=step):
            for part in range(len(parts)):
                block = block_at(part, step, count)
                transfer(part, block, step).wait_recv()
                for later in range(step + 1, group.bits):
                    transfer(part, block, later).start()
            return carried

        lax.fori_loop(0, 1 << step, arrived, 0)
    for copy in locals_:
        copy.wait()
    for step in range(group.bits):
        for part in range(len(parts)):
            transfer(part, me, step, True).wait_send()
    for step in range(group.bits - 1):

        def sent(count, carried, step=step):
            for part in range(len(parts)):
                block = block_at(part, step, count)
                for later in range(step + 1, group.bits):
                    transfer(part, block, later).wait_send()
            return carried

        lax.fori_loop(0, 1 << step, sent, 0)


def gather_all(group, parts, owns, collective_id):
    any_spec = pl.BlockSpec(memory_space=pl.ANY)
    return pl.pallas_call(
        functools.partial(gather_kernel, group, parts, len(owns)),
        out_shape=[jax.ShapeDtypeStruct((group.size,) + own.shape, own.dtype) for own in owns],
        in_specs=[any_spec] * len(owns),
        out_specs=[any_spec] * len(owns),
        scratch_shapes=[
            pltpu.SemaphoreType.DMA((len(owns),)),
            pltpu.SemaphoreType.DMA((len(parts), group.size)),
            pltpu.SemaphoreType.DMA((len(parts), group.size)),
        ],
        compiler_params=pltpu.CompilerParams(
            collective_id=collective_id, has_side_effects=True
        ),
    )(*owns)


def reduce_kernel(group, parts, piece_rows, array_count, *refs):
    piece_count = sum(len(rows) for rows in piece_rows)
    piece_refs = refs[:piece_count]
    out_refs = refs[piece_count : piece_count + array_count]
    refs = refs[piece_count + array_count :]
    term_refs, refs = refs[:array_count], refs[array_count:]
    held = [
        refs[part * group.bits : (part + 1) * group.bits] for part in range(len(parts))
    ]
    local_sem, send_sem, recv_sem = refs[len(parts) * group.bits :]
    me = group.position()
    copies = []
    for number in range(array_count):
        first = 0
        for rows in piece_rows[number]:
            copy = pltpu.make_async_copy(
                piece_refs[len(copies)],
                term_refs[number].at[pl.ds(first, rows)],
                local_sem.at[len(copies)],
            )
            copy.start()
            copies.append(copy)
            first += rows
    enter(group, me)
    for copy in copies:
        copy.wait()
    orders = [part[3] for part in parts]

    def source_of(part, step, block):
        number, first, count, _ = parts[part]
        if step == 0:
            each = term_refs[number].shape[0] // group.size
            start = pl.multiple_of(block * each + first, first_tile(first, each))
            return term_refs[number].at[pl.ds(start, count)]
        return held[part][step - 1].at[compress(block, orders[part][step:])]

    def transfer(part, step, block):
        slot = compress(block, orders[part][step + 1 :])
        return pltpu.make_async_remote_copy(
            src_ref=source_of(part, step, block),
            dst_ref=held[part][step].at[slot],
            send_sem=send_sem.at[part, block_count(step) + slot],
            recv_sem=recv_sem.at[part, block_count(step) + slot],
            device_id=group.place(flipped(me, orders[part][step])),
            device_id_type=pl.DeviceIdType.MESH,
        )

    def block_at(part, step, count, away):
        order = orders[part]
        block = flipped(me, order[step]) if away else me
        left = order[step + 1 :]
        for rank, bit in enumerate(left):
            chosen = bit_of(count, len(left) - 1 - rank)
            block = block + chosen * (1 - 2 * bit_of(me, bit)) * (1 << bit)
        return block

    def block_count(step):
        return 1 << (group.bits - 1 - step)

    def first_sends(index, carried):
        for part in range(len(parts)):
            transfer(part, 0, block_at(part, 0, block_count(0) - 1 - index, True)).start()
        return carried

    lax.fori_loop(0, block_count(0), first_sends, 0)
    for step in range(group.bits):
        total = block_count(step)
        last = step == group.bits - 1

        def arrived(index, carried, step=step, total=total, last=last, onward=True):
            for part in range(len(parts)):
                number, first, count, _ = parts[part]
                block = block_at(part, step, total - 1 - index, False)
                transfer(part, step, block).wait_recv()
                slot = compress(block, orders[part][step + 1 :])
                mine = source_of(part, step, block)[...].astype(jnp.float32)
                summed = held[part][step][slot].astype(jnp.float32) + mine
                if last:
                    out_refs[number][pl.ds(first, count), :] = summed
                else:
                    held[part][step][slot] = summed.astype(held[part][step].dtype)
                    if onward:
                        transfer(part, step + 1, block).start()
            return carried

        if last:
            arrived(0, 0)
        else:
            lax.fori_loop(0, total // 2, arrived, 0)
            lax.fori_loop(total // 2, total, functools.partial(arrived, onward=False), 0)
    for step in range(group.bits):

        def sent(count, carried, step=step):
            for part in range(len(parts)):
                transfer(part, step, block_at(part, step, count, True)).wait_send()
            return carried

        lax.fori_loop(0, block_count(step), sent, 0)


def first_tile(first, each):
    tile = ROW_TILE
    while first % tile or each % tile:
        tile //= 2
    return tile


def reduce_all(group, parts, pieces, collective_id):
    flat = [piece for array in pieces for piece in array]
    rows = [sum(piece.shape[0] for piece in array) for array in pieces]
    widths = [array[0].shape[1] for array in pieces]
    types = [array[0].dtype for array in pieces]
    return pl.pallas_call(
        functools.partial(
            reduce_kernel,
            group,
            parts,
            [[piece.shape[0] for piece in array] for array in pieces],
            len(pieces),
        ),
        out_shape=[
            jax.ShapeDtypeStruct((total // group.size, width), jnp.float32)
            for total, width in zip(rows, widths)
        ],
        in_specs=[pl.BlockSpec(memory_space=pl.ANY)] * len(flat),
        out_specs=[pl.BlockSpec(memory_space=pltpu.VMEM)] * len(pieces),
        scratch_shapes=[
            pltpu.VMEM((total, width), kind) for total, width, kind in zip(rows, widths, types)
        ]
        + [
            pltpu.VMEM((1 << (group.bits - 1 - step), count, widths[number]), types[number])
            for number, _, count, _ in parts
            for step in range(group.bits)
        ]
        + [
            pltpu.SemaphoreType.DMA((len(flat),)),
            pltpu.SemaphoreType.DMA((len(parts), group.size)),
            pltpu.SemaphoreType.DMA((len(parts), group.size)),
        ],
        compiler_params=pltpu.CompilerParams(
            collective_id=collective_id, has_side_effects=True, vmem_limit_bytes=56 << 20
        ),
    )(*flat)


def rms_apply(values, offset):
    scale_rows = lax.rsqrt(jnp.mean(values * values, axis=-1, keepdims=True) + NORM_EPS)
    return values * scale_rows * (1.0 + offset)


def norm_back(values, offset, upstream):
    _, pullback = jax.vjp(rms_apply, values, offset)
    return pullback(upstream)


def gated_unit(gate_values, up_values):
    return jax.nn.gelu(gate_values, approximate=True) * up_values


def rope_tables(token_pos):
    half_width = HD // 2
    exponents = jnp.arange(half_width, dtype=jnp.float32) * (2.0 / HD)
    frequency = jnp.power(jnp.float32(ROPE_BASE), -exponents)
    angles = token_pos.astype(jnp.float32)[:, None] * frequency[None, :]
    cosine_table = jnp.cos(angles)
    sine_table = jnp.sin(angles)
    return (
        jnp.concatenate([cosine_table, cosine_table], axis=-1),
        jnp.concatenate([sine_table, sine_table], axis=-1),
    )


def rotate(values, cosine_table, sine_table):
    half_width = values.shape[-1] // 2
    first_half = values[..., :half_width]
    second_half = values[..., half_width:]
    turned = jnp.concatenate([-second_half, first_half], axis=-1)
    return values * cosine_table + turned * sine_table


def rotate_back(upstream, cosine_table, sine_table):
    half_width = upstream.shape[-1] // 2
    weighted = upstream * sine_table
    turned = jnp.concatenate([weighted[..., half_width:], -weighted[..., :half_width]], axis=-1)
    return upstream * cosine_table + turned


def split_weights(row_values):
    width_qkv = HEADS * HD + 2 * HD
    first_end = D * width_qkv
    second_end = first_end + HEADS * HD * D
    third_end = second_end + 2 * D * FF
    return (
        row_values[: first_end // LANES].reshape(D, width_qkv),
        row_values[first_end // LANES : second_end // LANES].reshape(HEADS * HD, D),
        row_values[second_end // LANES : third_end // LANES].reshape(D, 2 * FF),
        row_values[third_end // LANES :].reshape(FF, D),
    )


def split_gains(flat_values):
    return (
        flat_values[:D],
        flat_values[D : D + HD],
        flat_values[D + HD : D + 2 * HD],
        flat_values[D + 2 * HD : 2 * D + 2 * HD],
        flat_values[2 * D + 2 * HD : 3 * D + 2 * HD],
        flat_values[3 * D + 2 * HD :],
    )


def adamw_update(weights, first_state, second_state, gradient):
    new_first = BETA_ONE * first_state + (1.0 - BETA_ONE) * gradient
    new_second = BETA_TWO * second_state + (1.0 - BETA_TWO) * gradient * gradient
    first_hat = new_first / (1.0 - BETA_ONE**STEP)
    second_hat = new_second / (1.0 - BETA_TWO**STEP)
    update = first_hat / (jnp.sqrt(second_hat) + ADAM_EPS) + DECAY_RATE * weights
    return (weights - LEARN_RATE * update, new_first, new_second)


def by_head(flat):
    return jnp.concatenate([flat[:, h * HD : (h + 1) * HD] for h in range(HEADS)], axis=0)


def attend_kernel(query_ref, keyval_ref, query_order_ref, key_order_ref, attn_ref, lse_ref, acc, tot):
    chunk = pl.program_id(0)

    @pl.when(chunk == 0)
    def _():
        acc[...] = jnp.zeros_like(acc)
        tot[...] = jnp.zeros_like(tot)

    keys, values = keyval_ref[:, :HD], keyval_ref[:, HD:]
    scores = lax.dot_general(
        by_head(query_ref[...]), keys, (((1,), (1,)), ((), ())), preferred_element_type=jnp.float32
    )
    weights = jnp.where(key_order_ref[...] <= query_order_ref[...], jnp.exp(scores), 0.0)
    tot[...] += jnp.sum(weights, axis=1, keepdims=True)
    acc[...] += jnp.dot(
        weights.astype(jnp.bfloat16), values, preferred_element_type=jnp.float32
    )

    @pl.when(chunk == pl.num_programs(0) - 1)
    def _():
        rows = attn_ref.shape[0]
        total = tot[...]
        result = (acc[...] / total).astype(jnp.bfloat16)
        for h in range(HEADS):
            attn_ref[:, h * HD : (h + 1) * HD] = result[h * rows : (h + 1) * rows]
        lse_ref[...] = jnp.log(total)


def attend_back_kernel(
    query_ref,
    grad_ref,
    keyval_ref,
    query_order_ref,
    key_order_ref,
    lse_ref,
    delta_ref,
    grad_query_ref,
    grad_keyval_ref,
    acc,
):
    chunk = pl.program_id(0)

    @pl.when(chunk == 0)
    def _():
        acc[...] = jnp.zeros_like(acc)

    keys, values = keyval_ref[:, :HD], keyval_ref[:, HD:]
    queries, grads = by_head(query_ref[...]), by_head(grad_ref[...])
    scores = lax.dot_general(
        keys, queries, (((1,), (1,)), ((), ())), preferred_element_type=jnp.float32
    )
    weights = jnp.where(
        key_order_ref[...] <= query_order_ref[...], jnp.exp(scores - lse_ref[...]), 0.0
    )
    grad_weights = lax.dot_general(
        values, grads, (((1,), (1,)), ((), ())), preferred_element_type=jnp.float32
    )
    grad_scores = (weights * (grad_weights - delta_ref[...])).astype(jnp.bfloat16)
    grad_keyval_ref[:, :HD] = jnp.dot(
        grad_scores, queries, preferred_element_type=jnp.float32
    ).astype(jnp.bfloat16)
    grad_keyval_ref[:, HD:] = jnp.dot(
        weights.astype(jnp.bfloat16), grads, preferred_element_type=jnp.float32
    ).astype(jnp.bfloat16)
    acc[...] += lax.dot_general(
        grad_scores, keys, (((0,), (0,)), ((), ())), preferred_element_type=jnp.float32
    )

    @pl.when(chunk == pl.num_programs(0) - 1)
    def _():
        rows = grad_query_ref.shape[0]
        for h in range(HEADS):
            grad_query_ref[:, h * HD : (h + 1) * HD] = acc[h * rows : (h + 1) * rows, :]


KEY_CHUNK = 1024


def fixed(shape):
    return pl.BlockSpec(shape, lambda i: (0,) * len(shape))


def attend(queries, keyval, query_order, key_order):
    rows, keys = queries.shape[0], keyval.shape[0]
    return pl.pallas_call(
        attend_kernel,
        grid=(keys // KEY_CHUNK,),
        out_shape=[
            jax.ShapeDtypeStruct((rows, HEADS * HD), jnp.bfloat16),
            jax.ShapeDtypeStruct((HEADS * rows, 1), jnp.float32),
        ],
        in_specs=[
            fixed((rows, HEADS * HD)),
            pl.BlockSpec((KEY_CHUNK, 2 * HD), lambda i: (i, 0)),
            fixed((HEADS * rows, 1)),
            pl.BlockSpec((1, KEY_CHUNK), lambda i: (0, i)),
        ],
        out_specs=[fixed((rows, HEADS * HD)), fixed((HEADS * rows, 1))],
        scratch_shapes=[
            pltpu.VMEM((HEADS * rows, HD), jnp.float32),
            pltpu.VMEM((HEADS * rows, 1), jnp.float32),
        ],
        compiler_params=pltpu.CompilerParams(vmem_limit_bytes=40 << 20),
    )(queries, keyval, query_order[:, None], key_order[None, :])


def attend_back(queries, grads, keyval, query_order, key_order, lse, delta):
    rows, keys = queries.shape[0], keyval.shape[0]
    row = fixed((1, HEADS * rows))
    return pl.pallas_call(
        attend_back_kernel,
        grid=(keys // KEY_CHUNK,),
        out_shape=[
            jax.ShapeDtypeStruct((rows, HEADS * HD), jnp.float32),
            jax.ShapeDtypeStruct((keys, 2 * HD), jnp.bfloat16),
        ],
        in_specs=[
            fixed((rows, HEADS * HD)),
            fixed((rows, HEADS * HD)),
            pl.BlockSpec((KEY_CHUNK, 2 * HD), lambda i: (i, 0)),
            row,
            pl.BlockSpec((KEY_CHUNK, 1), lambda i: (i, 0)),
            row,
            row,
        ],
        out_specs=[
            fixed((rows, HEADS * HD)),
            pl.BlockSpec((KEY_CHUNK, 2 * HD), lambda i: (i, 0)),
        ],
        scratch_shapes=[pltpu.VMEM((HEADS * rows, HD), jnp.float32)],
        compiler_params=pltpu.CompilerParams(vmem_limit_bytes=40 << 20),
    )(queries, grads, keyval, query_order[None, :], key_order[:, None], lse, delta)


def shards(
    inputs,
    cotangent,
    positions,
    block_map,
    matrices,
    gain_offsets,
    first_moment,
    second_moment,
    gain_first,
    gain_second,
):
    fsdp_size = lax.axis_size("fsdp")
    every = Group(lax.axis_size("ctx"), fsdp_size, True)
    sequence = Group(lax.axis_size("ctx"), fsdp_size, False)
    shard_rows = matrices.shape[0] // LANES
    padded_rows = -(-shard_rows // ROW_TILE) * ROW_TILE
    extra_rows = padded_rows - shard_rows
    (early, late), (order_a, order_b) = row_parts(padded_rows), every.orders()
    shard_parts = ((0,) + early + (order_a,), (0,) + late + (order_b,))
    gain_count = gain_offsets.shape[0]
    own_gains = jnp.pad(
        gain_offsets.astype(jnp.bfloat16).reshape(1, gain_count),
        ((0, ROW_TILE - 1), (0, LANES - gain_count)),
    )
    gathered, gain_rows = gather_all(
        every,
        shard_parts + ((1, 0, ROW_TILE, order_a),),
        [
            jnp.pad(
                matrices.astype(jnp.bfloat16).reshape(shard_rows, LANES), ((0, extra_rows), (0, 0))
            ),
            own_gains,
        ],
        0,
    )
    gathered = gathered[:, :shard_rows].reshape(-1, LANES)
    gains_low = gain_rows[:, 0, :gain_count].reshape(-1)
    w_qkv, w_out, w_gateup, w_down = split_weights(gathered)
    gain_in, gain_query, gain_key, gain_attn, gain_ffn, gain_post = split_gains(
        gains_low.astype(jnp.float32)
    )
    token_rows = inputs.shape[1]
    query_scale = HD ** (-0.5)
    residual_in = inputs[0]
    grad_output = cotangent[0]
    num_blocks = block_map.shape[0]
    block_ids = jnp.arange(num_blocks, dtype=jnp.int32)
    block_offsets = jnp.arange(BLK, dtype=jnp.int32)
    ctx_index = lax.axis_index("ctx")
    own_blocks = jnp.sum(
        jnp.where(
            (2 * ctx_index + jnp.arange(2, dtype=jnp.int32))[:, None] == block_ids[None, :],
            block_map[None, :],
            0,
        ),
        axis=1,
    )
    token_order = (own_blocks[:, None] * BLK + block_offsets[None, :]).reshape(token_rows)
    query_order = jnp.tile(token_order, HEADS)
    key_order = (block_map[:, None] * BLK + block_offsets[None, :]).reshape(num_blocks * BLK)
    cosine_table, sine_table = rope_tables(positions[0])
    normed_in = rms_apply(residual_in, gain_in).astype(jnp.bfloat16)
    projected = jnp.dot(normed_in, w_qkv, preferred_element_type=jnp.float32)
    query_raw = projected[:, : HEADS * HD].reshape(token_rows, HEADS, HD)
    key_raw = projected[:, HEADS * HD : HEADS * HD + HD]
    value_raw = projected[:, HEADS * HD + HD :]
    query_normed = rms_apply(query_raw, gain_query)
    key_normed = rms_apply(key_raw, gain_key)
    query_rows = (
        (rotate(query_normed, cosine_table[:, None], sine_table[:, None]) * query_scale)
        .astype(jnp.bfloat16)
        .reshape(token_rows, HEADS * HD)
    )
    own_keyval = jnp.concatenate(
        [rotate(key_normed, cosine_table, sine_table), value_raw], axis=1
    ).astype(jnp.bfloat16)
    (early_kv, late_kv), (order_c, order_d) = row_parts(token_rows, 8), sequence.orders()
    keyval_parts = ((0,) + early_kv + (order_c,), (0,) + late_kv + (order_d,))
    (all_keyval,) = gather_all(sequence, keyval_parts, [own_keyval], 2)
    all_keyval = all_keyval.reshape(num_blocks * BLK, 2 * HD)
    attn_flat, log_total = attend(query_rows, all_keyval, query_order, key_order)
    branch_attn = jnp.dot(attn_flat, w_out, preferred_element_type=jnp.float32)
    after_attn = residual_in + rms_apply(branch_attn, gain_attn)
    normed_mid = rms_apply(after_attn, gain_ffn).astype(jnp.bfloat16)
    gate_up = jnp.dot(normed_mid, w_gateup, preferred_element_type=jnp.float32)
    gate_values = gate_up[:, :FF]
    up_values = gate_up[:, FF:]
    hidden = gated_unit(gate_values, up_values).astype(jnp.bfloat16)
    branch_ffn = jnp.dot(hidden, w_down, preferred_element_type=jnp.float32)
    result = after_attn + rms_apply(branch_ffn, gain_post)
    grad_branch, grad_gain_post = norm_back(branch_ffn, gain_post, grad_output)
    grad_branch_low = grad_branch.astype(jnp.bfloat16)
    grad_down = jnp.dot(hidden.T, grad_branch_low, preferred_element_type=jnp.float32)
    grad_hidden = jnp.dot(grad_branch_low, w_down.T, preferred_element_type=jnp.float32)
    _, unit_pull = jax.vjp(gated_unit, gate_values, up_values)
    grad_gate, grad_up = unit_pull(grad_hidden)
    grad_gateup_low = jnp.concatenate([grad_gate, grad_up], axis=1).astype(jnp.bfloat16)
    grad_gateup = jnp.dot(normed_mid.T, grad_gateup_low, preferred_element_type=jnp.float32)
    grad_normed_mid = jnp.dot(grad_gateup_low, w_gateup.T, preferred_element_type=jnp.float32)
    grad_mid_part, grad_gain_ffn = norm_back(after_attn, gain_ffn, grad_normed_mid)
    grad_after = grad_output + grad_mid_part
    grad_attn_branch, grad_gain_attn = norm_back(branch_attn, gain_attn, grad_after)
    grad_attn_low = grad_attn_branch.astype(jnp.bfloat16)
    grad_wout = jnp.dot(attn_flat.T, grad_attn_low, preferred_element_type=jnp.float32)
    grad_rows = jnp.dot(grad_attn_low, w_out.T, preferred_element_type=jnp.float32).astype(
        jnp.bfloat16
    )
    delta_rows = jnp.sum(
        (grad_rows.astype(jnp.float32) * attn_flat.astype(jnp.float32)).reshape(
            token_rows, HEADS, HD
        ),
        axis=2,
    )
    grad_query_all, slot_terms = attend_back(
        query_rows,
        grad_rows,
        all_keyval,
        query_order,
        key_order,
        log_total.reshape(1, HEADS * token_rows),
        delta_rows.T.reshape(1, HEADS * token_rows),
    )
    (key_terms,) = reduce_all(
        sequence, keyval_parts, [[slot_terms]], 3
    )
    grad_key_rot = key_terms[:, :HD]
    grad_value = key_terms[:, HD:]
    grad_query_rot = grad_query_all.reshape(token_rows, HEADS, HD)
    grad_query_normed = rotate_back(
        grad_query_rot * query_scale, cosine_table[:, None], sine_table[:, None]
    )
    grad_query_raw, grad_gain_query = norm_back(query_raw, gain_query, grad_query_normed)
    grad_key_normed = rotate_back(grad_key_rot, cosine_table, sine_table)
    grad_key_raw, grad_gain_key = norm_back(key_raw, gain_key, grad_key_normed)
    grad_projected = jnp.concatenate(
        [grad_query_raw.reshape(token_rows, HEADS * HD), grad_key_raw, grad_value], axis=1
    ).astype(jnp.bfloat16)
    grad_wqkv = jnp.dot(normed_in.T, grad_projected, preferred_element_type=jnp.float32)
    grad_normed_in = jnp.dot(grad_projected, w_qkv.T, preferred_element_type=jnp.float32)
    grad_in_part, grad_gain_in = norm_back(residual_in, gain_in, grad_normed_in)
    grad_input = grad_after + grad_in_part
    local_gain = jnp.concatenate(
        [
            grad_gain_in,
            grad_gain_query,
            grad_gain_key,
            grad_gain_attn,
            grad_gain_ffn,
            grad_gain_post,
        ]
    )
    gain_terms = jnp.pad(
        local_gain.reshape(every.size, 1, gain_count), ((0, 0), (0, 7), (0, LANES - gain_count))
    ).reshape(every.size * 8, LANES)
    matrix_terms = [
        term.astype(jnp.bfloat16).reshape(-1, LANES)
        for term in (grad_wqkv, grad_wout, grad_gateup, grad_down)
    ]
    if extra_rows:
        whole_terms = jnp.concatenate(matrix_terms).reshape(every.size, shard_rows, LANES)
        matrix_terms = [
            jnp.pad(whole_terms, ((0, 0), (0, extra_rows), (0, 0))).reshape(-1, LANES)
        ]
    matrix_rows, gain_sums = reduce_all(
        every, shard_parts + ((1, 0, 8, order_a),), [matrix_terms, [gain_terms]], 1
    )
    matrix_grad = matrix_rows[:shard_rows].reshape(-1)
    gain_grad = gain_sums[0, :gain_count]
    new_matrices, new_first, new_second = adamw_update(
        matrices, first_moment, second_moment, matrix_grad
    )
    new_gains, new_gain_first, new_gain_second = adamw_update(
        gain_offsets, gain_first, gain_second, gain_grad
    )
    return (
        result[None],
        grad_input[None],
        matrix_grad,
        gain_grad,
        new_matrices,
        new_gains,
        new_first,
        new_second,
        new_gain_first,
        new_gain_second,
    )


def solution(mesh):
    return jax.shard_map(
        shards,
        mesh=mesh,
        in_specs=(
            P("fsdp", "ctx", None),
            P("fsdp", "ctx", None),
            P("fsdp", "ctx"),
            P(),
            P(("ctx", "fsdp")),
            P(("ctx", "fsdp")),
            P(("ctx", "fsdp")),
            P(("ctx", "fsdp")),
            P(("ctx", "fsdp")),
            P(("ctx", "fsdp")),
        ),
        out_specs=(
            P("fsdp", "ctx", None),
            P("fsdp", "ctx", None),
            P(("ctx", "fsdp")),
            P(("ctx", "fsdp")),
            P(("ctx", "fsdp")),
            P(("ctx", "fsdp")),
            P(("ctx", "fsdp")),
            P(("ctx", "fsdp")),
            P(("ctx", "fsdp")),
            P(("ctx", "fsdp")),
        ),
        check_vma=False,
    )
```
